256 devices in a mesh: depth: 8 (over x, z_lo), map: 32 (over z_hi, y, core).
Axes of the slice: x: 4, y: 4, z: 8 (z_hi: 4, z_lo: 2; z = z_hi * 2 + z_lo), core: 2. Of those that a mesh axis runs over, the one named last changes fastest.
Arguments:
- velocity: float32 [3, 128, 1024, 128], P(None, 'depth', 'map'), may hold values from -6 to 6
- stress: float32 [6, 128, 1024, 128], P(None, 'depth', 'map'), may hold values from -6 to 6
- region: int32 [128, 1024, 128], P('depth', 'map'), may hold values from 0 to 7
- lame_table: float32 [8], replicated, may hold values from 0.2 to 0.5
- shear_table: float32 [8], replicated, may hold values from 0.1 to 0.3
- buoyancy_table: float32 [8], replicated, may hold values from 0.6 to 1.2
- height: float32 [1024, 8192], P('depth', 'map'), may hold values from -6 to 6
- discharge: float32 [2, 1024, 8192], P(None, 'depth', 'map'), may hold values from -6 to 6
- face_depth: float32 [2, 1024, 8192], P(None, 'depth', 'map'), may hold values from 0.5 to 2
- wet: int32 [1024, 8192], P('depth', 'map'), may hold values 0 or 1
- seafloor_index: int32 [1024, 8192], P('depth', 'map'), may hold values from 0 to 4095
Outputs:
- velocity_out: float32 [3, 128, 1024, 128], P(None, 'depth', 'map')
- stress_out: float32 [6, 128, 1024, 128], P(None, 'depth', 'map')
- height_out: float32 [1024, 8192], P('depth', 'map')
- discharge_out: float32 [2, 1024, 8192], P(None, 'depth', 'map')
The draws below stay inside these ranges and needn't reach their ends.
Inputs may be any that keep to these rules, and one draw needn't show every extreme that they name: `wet`: 1 for a wet ocean cell, 0 for a dry one. `seafloor_index`: index k of the seafloor cell under an ocean cell, among the 32 x 128 crust cells of its own map column, counted row by row.
All inputs are finite; a program needn't handle non-finite values. No bound on the sum of `wet` on one device may be relied on, other than what follows from the above.
Results may differ from the reference program's by a relative error of at most 0.000054.
Values sent between devices are 32-bit elements; how exact they have to be, the bound alone decides.
A program may use at most 64 MiB of HBM per device.

```python
import math
import jax
import jax.numpy as jnp
from jax import lax

CX = 32
NY = 128
REGIONS = 8
ITERS = 3
OC = 256
OSTEPS = 2
NZ = 128
NX = 1024
NOR = 1024
NOC = 8192


def plant(drawn, stream_key, least, high):
    index_at = [jax.random.randint(jax.random.fold_in(stream_key, axis), (), 0, length) for axis, length in enumerate(drawn.shape)]
    widest = drawn.shape.index(max(drawn.shape))
    beside = index_at[:widest] + [(index_at[widest] + 1) % drawn.shape[widest]] + index_at[widest + 1:]
    return drawn.at[tuple(index_at)].set(least).at[tuple(beside)].set(high)


def levels(stream_key, shape, pieces, least, largest):
    gain, own = 1.0, jax.random.fold_in(stream_key, 6)
    for dim, blocks in pieces:
        steps = jnp.exp(jax.random.uniform(jax.random.fold_in(own, dim), (blocks,), jnp.float32, least / len(pieces), largest / len(pieces)))
        gain = gain * jnp.repeat(steps, shape[dim] // blocks).reshape([-1 if axis == dim else 1 for axis in range(len(shape))])
    return gain


def bell_draw(stream_key, shape, scale, reach, shards=(), kind=jnp.bfloat16):
    factor_of = levels(stream_key, shape, shards, -0.22, 0.18) if shards else 1.0
    array = jax.random.normal(stream_key, shape, jnp.float32) * scale * factor_of
    return jnp.minimum(jnp.maximum(array, -reach), reach).astype(kind)


def setup_inputs(seed: int = 0) -> dict:
    seeds = jax.random.split(jax.random.key(seed), 12)
    return {
        "velocity": bell_draw(seeds[0], (3, NZ, NX, NY), 1.0, 6.0, ((1, 8), (2, 32)), jnp.float32),
        "stress": bell_draw(seeds[1], (6, NZ, NX, NY), 1.0, 6.0, ((1, 8), (2, 32)), jnp.float32),
        "region": plant(jax.random.randint(seeds[2], (NZ, NX, NY), 0, REGIONS), jax.random.fold_in(seeds[2], 1), 0, REGIONS - 1).astype(jnp.int32),
        "lame_table": jnp.clip(jax.random.uniform(seeds[3], (REGIONS,), jnp.float32, 0.2, 0.5), 0.2, 0.5),
        "shear_table": jnp.clip(jax.random.uniform(seeds[4], (REGIONS,), jnp.float32, 0.1, 0.3), 0.1, 0.3),
        "buoyancy_table": jnp.clip(jax.random.uniform(seeds[5], (REGIONS,), jnp.float32, 0.6, 1.2), 0.6, 1.2),
        "height": bell_draw(seeds[6], (NOR, NOC), 1.0, 6.0, ((0, 8), (1, 32)), jnp.float32),
        "discharge": bell_draw(seeds[7], (2, NOR, NOC), 1.0, 6.0, ((1, 8), (2, 32)), jnp.float32),
        "face_depth": jnp.clip(jnp.exp(math.log(2.0) - 1.3862944 * jax.random.uniform(seeds[8], (2, NOR, NOC), jnp.float32) ** levels(seeds[8], (2, NOR, NOC), ((1, 8), (2, 32)), -0.2, 0.2)), 0.5, 2.0),
        "wet": plant((jax.random.randint(seeds[9], (NOR, NOC), 0, 4) < 3).astype(jnp.int32), jax.random.fold_in(seeds[9], 1), 0, 1),
        "seafloor_index": plant(jax.random.randint(seeds[10], (NOR, NOC), 0, CX * NY), jax.random.fold_in(seeds[10], 1), 0, (CX * NY) - 1).astype(jnp.int32),
    }


near_coef = 9.0 / 8.0
far_coef = 1.0 / 24.0
time_step = 0.2
ocean_step = 0.2
gravity = 1.0


def cells(padded, axis, offset, count):
    return lax.slice_in_dim(padded, offset, offset + count, axis=axis)


def forward_diff(padded, axis):
    count = padded.shape[axis] - 4
    return near_coef * (cells(padded, axis, 3, count) - cells(padded, axis, 2, count)) - far_coef * (cells(padded, axis, 4, count) - cells(padded, axis, 1, count))


def backward_diff(padded, axis):
    count = padded.shape[axis] - 4
    return near_coef * (cells(padded, axis, 2, count) - cells(padded, axis, 1, count)) - far_coef * (cells(padded, axis, 3, count) - cells(padded, axis, 0, count))


def forward_y(field):
    return near_coef * (jnp.roll(field, -1, 2) - field) - far_coef * (jnp.roll(field, -2, 2) - jnp.roll(field, 1, 2))


def backward_y(field):
    return near_coef * (field - jnp.roll(field, 1, 2)) - far_coef * (jnp.roll(field, -1, 2) - jnp.roll(field, 2, 2))


def pad_map(field):
    return jnp.pad(field, ((0, 0), (2, 2), (0, 0)))


def pad_depth(field):
    return jnp.pad(field, ((2, 2), (0, 0), (0, 0)))


def reference(velocity, stress, region, lame_table, shear_table, buoyancy_table, height, discharge, face_depth, wet, seafloor_index):
    lame = jnp.take(lame_table, region)
    shear = jnp.take(shear_table, region)
    buoyancy = jnp.take(buoyancy_table, region)
    speeds = [velocity[0], velocity[1], velocity[2]]
    forces = [stress[index] for index in range(6)]
    lift = jnp.zeros((velocity.shape[2], velocity.shape[3]), jnp.float32)
    for turn in range(ITERS):
        speed_x = speeds[0] + time_step * buoyancy * (forward_diff(pad_map(forces[0]), 1) + backward_y(forces[1]) + backward_diff(pad_depth(forces[2]), 0))
        speed_y = speeds[1] + time_step * buoyancy * (backward_diff(pad_map(forces[1]), 1) + forward_y(forces[5]) + backward_diff(pad_depth(forces[3]), 0))
        speed_z = speeds[2] + time_step * buoyancy * (backward_diff(pad_map(forces[2]), 1) + backward_y(forces[3]) + forward_diff(pad_depth(forces[4]), 0))
        speeds = [speed_x, speed_y, speed_z]
        lift = lift + time_step * speed_z[0]
        strain_x = backward_diff(pad_map(speed_x), 1)
        strain_y = backward_y(speed_y)
        strain_z = backward_diff(pad_depth(speed_z), 0)
        spread = strain_x + strain_y + strain_z
        forces = [
            forces[0] + time_step * (lame * spread + 2.0 * shear * strain_x),
            forces[1] + time_step * shear * (forward_y(speed_x) + forward_diff(pad_map(speed_y), 1)),
            forces[2] + time_step * shear * (forward_diff(pad_depth(speed_x), 0) + forward_diff(pad_map(speed_z), 1)),
            forces[3] + time_step * shear * (forward_diff(pad_depth(speed_y), 0) + forward_y(speed_z)),
            forces[4] + time_step * (lame * spread + 2.0 * shear * strain_z),
            forces[5] + time_step * (lame * spread + 2.0 * shear * strain_y),
        ]
    rate = speeds[2][0]
    tile_size = CX * NY
    column = (jnp.arange(NOC, dtype=jnp.int32) // OC) * tile_size
    where = seafloor_index + column[None, :]
    lift_at = jnp.take(lift.reshape(-1), where)
    rate_at = jnp.take(rate.reshape(-1), where)
    wetness = wet.astype(jnp.float32)
    level = wetness * (height + lift_at)
    source = wetness * rate_at
    zero_col = jnp.zeros((NOR, 1), jnp.float32)
    zero_row = jnp.zeros((1, NOC), jnp.float32)
    wet_east = jnp.concatenate([wetness[:, 1:], zero_col], axis=1)
    wet_north = jnp.concatenate([wetness[1:, :], zero_row], axis=0)
    mask_x = wetness * wet_east
    mask_y = wetness * wet_north
    depth_x = face_depth[0] * mask_x
    depth_y = face_depth[1] * mask_y
    flux_x = discharge[0] * mask_x
    flux_y = discharge[1] * mask_y
    for turn in range(OSTEPS):
        level_east = jnp.concatenate([level[:, 1:], zero_col], axis=1)
        level_north = jnp.concatenate([level[1:, :], zero_row], axis=0)
        flux_x = flux_x - ocean_step * gravity * depth_x * (level_east - level)
        flux_y = flux_y - ocean_step * gravity * depth_y * (level_north - level)
        flux_west = jnp.concatenate([zero_col, flux_x[:, :-1]], axis=1)
        flux_south = jnp.concatenate([zero_row, flux_y[:-1, :]], axis=0)
        level = level - ocean_step * wetness * ((flux_x - flux_west) + (flux_y - flux_south)) + ocean_step * source
    return jnp.stack(speeds), jnp.stack(forces), level, jnp.stack([flux_x, flux_y])
```

```python
import jax
import jax.numpy as jnp
from jax import lax
from jax.experimental import pallas as pl
from jax.experimental.pallas import tpu as pltpu
from jax.sharding import PartitionSpec as P

ITERS = 3
OSTEPS = 2

far_coef = 1.0 / 24.0
RATIO = 27.0
time_step = 0.2
ocean_step = 0.2
gravity = 1.0
pull = ocean_step * gravity

LANES = 128
ROW0 = 8
XX, XY, XZ, YZ, ZZ, YY = range(6)
S_DEPTH = ((XZ, YZ + 1, True), (ZZ, ZZ + 1, False))
V_DEPTH = ((0, 2, False), (2, 3, True))
S_MAP = ((XX, False), (XY, True), (XZ, True))
V_MAP = ((0, True), (1, False), (2, False))


def turn_lanes(x, by):
    return pltpu.roll(x, by % LANES, 1)


def fwd(p1, c, p2, m1):
    return p1 - c, p2 - m1


def bwd(c, m1, p1, m2):
    return c - m1, p1 - m2


def fwd_y(f):
    return fwd(turn_lanes(f, -1), f, turn_lanes(f, -2), turn_lanes(f, 1))


def bwd_y(f):
    return bwd(f, turn_lanes(f, 1), turn_lanes(f, -1), turn_lanes(f, 2))


def scaled(*pairs):
    near, far = pairs[0]
    for n, f in pairs[1:]:
        near, far = near + n, far + f
    return RATIO * near - far


def up_slots(fields):
    out = []
    for field, back in fields:
        for k in (2, 1) if back else (1,):
            out.append((field, -k, -k))
    return out


def down_slots(fields):
    out = []
    for field, back in fields:
        for k in (0,) if back else (0, 1):
            out.append((field, k, k))
    return out


def kernel(
    n_depth,
    n_map,
    nz,
    nx,
    rows,
    vel_in,
    str_in,
    reg_in,
    lame_in,
    shear_in,
    buoy_in,
    height_in,
    disch_in,
    face_in,
    wet_in,
    index_in,
    vel_out,
    str_out,
    height_out,
    disch_out,
    S,
    V,
    region,
    dtb,
    dtl,
    dts,
    su_send,
    sd_send,
    su_recv,
    sd_recv,
    vu_send,
    vd_send,
    vu_recv,
    vd_recv,
    tiles,
    level,
    W,
    wet_i,
    index,
    height,
    qx,
    hx,
    fd0,
    qy,
    hy,
    fd1,
    source,
    lift2,
    col_send,
    col_recv,
    qw,
    hw,
    lame_t,
    shear_t,
    buoy_t,
    in_sem,
    out_sem,
    s_send_sem,
    s_recv_sem,
    v_send_sem,
    v_recv_sem,
    t_send_sem,
    t_recv_sem,
    o_send_sem,
    o_recv_sem,
):
    d = lax.axis_index("depth")
    m = lax.axis_index("map")
    has_low, has_high = d > 0, d < n_depth - 1
    has_west, has_east = m > 0, m < n_map - 1
    low, high = {"depth": d - 1, "map": m}, {"depth": d + 1, "map": m}
    west, east = {"depth": d, "map": m - 1}, {"depth": d, "map": m + 1}
    sides = ((has_low, low), (has_high, high), (has_west, west), (has_east, east))
    f32 = jnp.float32
    halves = range(2)

    s_loads = [
        pltpu.make_async_copy(
            str_in.at[f], S.at[f, pl.ds(2, nz), pl.ds(ROW0, nx), :], in_sem.at[f]
        )
        for f in range(6)
    ]
    r_loads = [
        pltpu.make_async_copy(src, dst, in_sem.at[k])
        for src, dst, k in (
            (reg_in, region, 6),
            (lame_in, lame_t, 24),
            (shear_in, shear_t, 25),
            (buoy_in, buoy_t, 26),
        )
    ]
    v_loads = [
        pltpu.make_async_copy(
            vel_in.at[f], V.at[f, pl.ds(2, nz), pl.ds(ROW0, nx), :], in_sem.at[7 + f]
        )
        for f in range(3)
    ]
    o_loads = []

    def half_load(src, dst):
        o_loads.append(pltpu.make_async_copy(src, dst, in_sem.at[10 + len(o_loads)]))

    for h in halves:
        cols = pl.ds(h * LANES, LANES)
        half_load(wet_in.at[:, cols], wet_i.at[h])
        half_load(index_in.at[:, cols], index.at[h])
        half_load(height_in.at[:, cols], height.at[h])
        half_load(disch_in.at[0, :, cols], qx.at[h])
        half_load(disch_in.at[1, :, cols], qy.at[h, pl.ds(8, rows), :])
        half_load(face_in.at[0, :, cols], fd0.at[h])
        half_load(face_in.at[1, :, cols], fd1.at[h, pl.ds(8, rows), :])
    for c in s_loads + r_loads + v_loads + o_loads:
        c.start()

    def clear_layers(z):
        for f in (XZ, YZ, ZZ):
            S[f, pl.ds(z, 2), pl.ds(ROW0, nx), :] = jnp.zeros((2, nx, LANES), f32)
        for f in range(3):
            V[f, pl.ds(z, 2), pl.ds(ROW0, nx), :] = jnp.zeros((2, nx, LANES), f32)

    @pl.when(d == 0)
    def _():
        clear_layers(0)

    @pl.when(d == n_depth - 1)
    def _():
        clear_layers(nz + 2)

    @pl.when(m == 0)
    def _():
        for ref in (su_recv, vu_recv):
            ref[...] = jnp.zeros(ref.shape, f32)

    @pl.when(m == n_map - 1)
    def _():
        for ref in (sd_recv, vd_recv):
            ref[...] = jnp.zeros(ref.shape, f32)

    for h in halves:
        for t in range(OSTEPS):
            level[t, h, pl.ds(0, 8), :] = jnp.zeros((8, LANES), f32)
            level[t, h, pl.ds(rows + 8, 8), :] = jnp.zeros((8, LANES), f32)
        W[h, pl.ds(0, 8), :] = jnp.zeros((8, LANES), f32)
        W[h, pl.ds(rows + 8, 8), :] = jnp.zeros((8, LANES), f32)
        qy[h, pl.ds(0, 8), :] = jnp.zeros((8, LANES), f32)
        fd1[h, pl.ds(0, 8), :] = jnp.zeros((8, LANES), f32)
    for k in range(3 + OSTEPS):
        col_recv[k] = jnp.zeros((LANES, LANES), f32)

    barrier = pltpu.get_barrier_semaphore()
    for there, who in sides:
        @pl.when(there)
        def _():
            pl.semaphore_signal(barrier, inc=1, device_id=who, device_id_type=pl.DeviceIdType.MESH)

    @pl.when(d > 1)
    def _():
        pl.semaphore_signal(
            barrier, inc=1, device_id={"depth": 0, "map": m}, device_id_type=pl.DeviceIdType.MESH
        )

    peers = sum(there.astype(jnp.int32) for there, _who in sides)
    pl.semaphore_wait(barrier, peers + jnp.where(d == 0, max(n_depth - 2, 0), 0))

    def remote(src, dst, ssem, rsem, who):
        return pltpu.make_async_remote_copy(
            src_ref=src,
            dst_ref=dst,
            send_sem=ssem,
            recv_sem=rsem,
            device_id=who,
            device_id_type=pl.DeviceIdType.MESH,
        )

    def over(lo, hi, body, at_once=1):
        def step(i, _):
            for k in range(at_once):
                body(lo + i * at_once + k)
            return 0

        lax.fori_loop(0, (hi - lo) // at_once, step, 0)

    xs = pl.ds(ROW0, nx)

    def depth_copies(ref, fields, ssem, rsem):
        ups, downs = [], []
        for k, (lo, hi, back) in enumerate(fields):
            n_up, n_down = (2, 1) if back else (1, 2)
            fs = pl.ds(lo, hi - lo)
            ups.append(
                remote(
                    ref.at[fs, pl.ds(nz + 2 - n_up, n_up), xs, :],
                    ref.at[fs, pl.ds(2 - n_up, n_up), xs, :],
                    ssem.at[k],
                    rsem.at[k],
                    high,
                )
            )
            downs.append(
                remote(
                    ref.at[fs, pl.ds(2, n_down), xs, :],
                    ref.at[fs, pl.ds(nz + 2, n_down), xs, :],
                    ssem.at[2 + k],
                    rsem.at[2 + k],
                    low,
                )
            )
        return ups, downs

    s_up, s_down = depth_copies(S, S_DEPTH, s_send_sem, s_recv_sem)
    v_up, v_down = depth_copies(V, V_DEPTH, v_send_sem, v_recv_sem)
    s_east = [remote(su_send, su_recv, s_send_sem.at[4], s_recv_sem.at[4], east)]
    s_west = [remote(sd_send, sd_recv, s_send_sem.at[5], s_recv_sem.at[5], west)]
    v_east = [remote(vu_send, vu_recv, v_send_sem.at[4], v_recv_sem.at[4], east)]
    v_west = [remote(vd_send, vd_recv, v_send_sem.at[5], v_recv_sem.at[5], west)]
    S_PLAN = (S, S_MAP, s_up, s_down, s_east, s_west, su_send, sd_send, su_recv, sd_recv)
    V_PLAN = (V, V_MAP, v_up, v_down, v_east, v_west, vu_send, vd_send, vu_recv, vd_recv)

    def each(there, copies, what):
        @pl.when(there)
        def _():
            for c in copies:
                getattr(c, what)()

    def send_depth(plan):
        each(has_high, plan[2], "start")
        each(has_low, plan[3], "start")

    def send_map(plan):
        ref, fields, _, _, east_c, west_c, u_send, d_send, _, _ = plan

        def pack(i):
            for j, (f, row, _r) in enumerate(up_slots(fields)):
                u_send[j, pl.ds(i, 1), :] = ref[f, i + 2, pl.ds(ROW0 + nx + row, 1), :]
            for j, (f, row, _r) in enumerate(down_slots(fields)):
                d_send[j, pl.ds(i, 1), :] = ref[f, i + 2, pl.ds(ROW0 + row, 1), :]

        over(0, nz, pack, 4)
        each(has_east, east_c, "start")
        each(has_west, west_c, "start")

    def take_map(plan):
        ref, fields, _, _, east_c, west_c, _, _, u_recv, d_recv = plan

        each(has_west, east_c, "wait_recv")
        each(has_east, west_c, "wait_recv")

        def unpack(i):
            for j, (f, _row, row) in enumerate(up_slots(fields)):
                ref[f, i + 2, pl.ds(ROW0 + row, 1), :] = u_recv[j, pl.ds(i, 1), :]
            for j, (f, _row, row) in enumerate(down_slots(fields)):
                ref[f, i + 2, pl.ds(ROW0 + nx + row, 1), :] = d_recv[j, pl.ds(i, 1), :]

        over(0, nz, unpack, 4)

    def take_depth(plan):
        each(has_low, plan[2], "wait_recv")
        each(has_high, plan[3], "wait_recv")

    def wait_sends(plan):
        each(has_high, plan[2], "wait_send")
        each(has_low, plan[3], "wait_send")
        each(has_east, plan[4], "wait_send")
        each(has_west, plan[5], "wait_send")

    def velocity_rows(z, a, b):
        def s(f, dz, dx):
            return S[f, z + 2 + dz, pl.ds(ROW0 + a + dx, b - a), :]

        def v_add(f, total):
            at = (f, z + 2, pl.ds(ROW0 + a, b - a), slice(None))
            V[at] = V[at] + dtb[z, pl.ds(a, b - a), :] * total

        xy, xz, yz = s(XY, 0, 0), s(XZ, 0, 0), s(YZ, 0, 0)
        v_add(
            0,
            scaled(
                fwd(s(XX, 0, 1), s(XX, 0, 0), s(XX, 0, 2), s(XX, 0, -1)),
                bwd_y(xy),
                bwd(xz, s(XZ, -1, 0), s(XZ, 1, 0), s(XZ, -2, 0)),
            ),
        )
        v_add(
            1,
            scaled(
                bwd(xy, s(XY, 0, -1), s(XY, 0, 1), s(XY, 0, -2)),
                fwd_y(s(YY, 0, 0)),
                bwd(yz, s(YZ, -1, 0), s(YZ, 1, 0), s(YZ, -2, 0)),
            ),
        )
        v_add(
            2,
            scaled(
                bwd(xz, s(XZ, 0, -1), s(XZ, 0, 1), s(XZ, 0, -2)),
                bwd_y(yz),
                fwd(s(ZZ, 1, 0), s(ZZ, 0, 0), s(ZZ, 2, 0), s(ZZ, -1, 0)),
            ),
        )

    def stress_rows(z, a, b):
        def v(f, dz, dx):
            return V[f, z + 2 + dz, pl.ds(ROW0 + a + dx, b - a), :]

        def s_add(f, change):
            at = (f, z + 2, pl.ds(ROW0 + a, b - a), slice(None))
            S[at] = S[at] + change

        x, y, w = v(0, 0, 0), v(1, 0, 0), v(2, 0, 0)
        ex = scaled(bwd(x, v(0, 0, -1), v(0, 0, 1), v(0, 0, -2)))
        ey = scaled(bwd_y(y))
        ez = scaled(bwd(w, v(2, -1, 0), v(2, 1, 0), v(2, -2, 0)))
        mu = dts[z, pl.ds(a, b - a), :]
        both = dtl[z, pl.ds(a, b - a), :] * (ex + ey + ez)
        mu2 = mu + mu
        s_add(XX, both + mu2 * ex)
        s_add(YY, both + mu2 * ey)
        s_add(ZZ, both + mu2 * ez)
        s_add(XY, mu * scaled(fwd_y(x), fwd(v(1, 0, 1), y, v(1, 0, 2), v(1, 0, -1))))
        s_add(
            XZ,
            mu
            * scaled(
                fwd(v(0, 1, 0), x, v(0, 2, 0), v(0, -1, 0)),
                fwd(v(2, 0, 1), w, v(2, 0, 2), v(2, 0, -1)),
            ),
        )
        s_add(YZ, mu * scaled(fwd(v(1, 1, 0), y, v(1, 2, 0), v(1, -1, 0)), fwd_y(w)))

    def inner(rows_of):
        over(2, nz - 2, lambda z: rows_of(z, 8, nx - 8), 2)

    def beside(rows_of):
        def body(z):
            rows_of(z, 0, 8)
            rows_of(z, nx - 8, nx)

        over(2, nz - 2, body, 2)

    def outer(rows_of):
        def body(i):
            rows_of(i, 0, nx)
            rows_of(i + nz - 2, 0, nx)

        over(0, 2, body)

    for c in s_loads:
        c.wait()
    send_depth(S_PLAN)
    send_map(S_PLAN)

    for c in r_loads:
        c.wait()
    lame = [lame_t[k] * (time_step * far_coef) for k in range(8)]
    shear = [shear_t[k] * (time_step * far_coef) for k in range(8)]
    buoy = [buoy_t[k] * (time_step * far_coef) for k in range(8)]

    def material(z):
        r = region[z]
        bit0, bit1, bit2 = (r & 1) > 0, (r & 2) > 0, (r & 4) > 0
        for table, out in ((lame, dtl), (shear, dts), (buoy, dtb)):
            a = [jnp.where(bit0, table[2 * k + 1], table[2 * k]) for k in range(4)]
            b = [jnp.where(bit1, a[2 * k + 1], a[2 * k]) for k in range(2)]
            out[z] = jnp.where(bit2, b[1], b[0])

    over(0, nz, material)
    for c in v_loads:
        c.wait()

    lane = lax.broadcasted_iota(jnp.int32, (rows, LANES), 1)
    first, last = lane == 0, lane == LANES - 1
    own = pl.ds(8, rows)

    def row_copies(ref, k, both):
        out = [
            (
                has_high,
                has_low,
                remote(
                    ref.at[:, pl.ds(rows, 8), :],
                    ref.at[:, pl.ds(0, 8), :],
                    o_send_sem.at[k],
                    o_recv_sem.at[k],
                    high,
                ),
            )
        ]
        if both:
            out.append(
                (
                    has_low,
                    has_high,
                    remote(
                        ref.at[:, pl.ds(8, 8), :],
                        ref.at[:, pl.ds(rows + 8, 8), :],
                        o_send_sem.at[k + 1],
                        o_recv_sem.at[k + 1],
                        low,
                    ),
                )
            )
        return out

    def col_copies(slot, k, both):
        tail = pl.ds(LANES - 8, 8)
        out = [
            (
                has_east,
                has_west,
                remote(
                    col_send.at[slot, tail, :],
                    col_recv.at[slot, tail, :],
                    o_send_sem.at[k],
                    o_recv_sem.at[k],
                    east,
                ),
            )
        ]
        if both:
            head = pl.ds(0, 8)
            out.append(
                (
                    has_west,
                    has_east,
                    remote(
                        col_send.at[slot, head, :],
                        col_recv.at[slot, head, :],
                        o_send_sem.at[k + 1],
                        o_recv_sem.at[k + 1],
                        west,
                    ),
                )
            )
        return out

    def start_all(copies):
        for there, _from, c in copies:
            each(there, [c], "start")

    def recv_all(copies):
        for _there, came, c in copies:
            each(came, [c], "wait_recv")

    def sent_all(copies):
        for there, _from, c in copies:
            each(there, [c], "wait_send")

    for c in o_loads:
        c.wait()
    for h in halves:
        W[h, own, :] = wet_i[h].astype(f32)
    col_send[0] = jnp.where(first, W[0, own, :], W[1, own, :]).T
    col_send[1] = fd0[1].T
    col_send[2] = qx[1].T
    fixed = (
        row_copies(W, 0, True)
        + row_copies(fd1, 2, False)
        + row_copies(qy, 3, False)
        + col_copies(0, 4, True)
        + col_copies(1, 6, False)
        + col_copies(2, 7, False)
    )
    start_all(fixed)

    def east_of(x0, x1, edge):
        r1 = turn_lanes(x1, -1)
        return (
            jnp.where(last, r1, turn_lanes(x0, -1)),
            jnp.where(last, turn_lanes(edge, -1), r1),
        )

    def west_of(x0, x1, edge):
        r0 = turn_lanes(x0, 1)
        return (
            jnp.where(first, turn_lanes(edge, 1), r0),
            jnp.where(first, r0, turn_lanes(x1, 1)),
        )

    def ocean_fixed():
        recv_all(fixed)
        sent_all(fixed)
        edge = col_recv[0].T
        w = (W[0, own, :], W[1, own, :])
        w_east = east_of(w[0], w[1], edge)
        wide = pl.ds(0, rows + 8)
        for h in halves:
            mask = w[h] * w_east[h]
            hx[h] = fd0[h] * mask
            qx[h] = qx[h] * mask
            mask = W[h, wide, :] * W[h, pl.ds(1, rows + 8), :]
            hy[h] = fd1[h] * mask
            qy[h] = qy[h] * mask
        mask = edge * turn_lanes(w[0], -1)
        hw[...] = col_recv[1].T * mask
        qw[...] = col_recv[2].T * mask

    def tile_copies(k):
        return [
            remote(
                tiles.at[k],
                tiles.at[k],
                t_send_sem.at[k * (n_depth - 1) + i],
                t_recv_sem.at[k],
                {"depth": i + 1, "map": m},
            )
            for i in range(n_depth - 1)
        ]

    sends = [tile_copies(0), tile_copies(1)]

    def send_tile(k):
        if n_depth > 1:
            each(d == 0, sends[k], "start")

    def take_tile(k):
        if n_depth > 1:
            each(d > 0, sends[k][:1], "wait_recv")

    def pick(k, take):
        def body(i):
            at = pl.ds(i * 8, 8)
            where = [index[h, at, :] for h in halves]
            lane_at = [x & (LANES - 1) for x in where]
            row_at = [x >> 7 for x in where]
            found = [[], []]
            for r in range(nx):
                line = jnp.broadcast_to(tiles[k, pl.ds(r, 1), :], (8, LANES))
                for h in halves:
                    found[h].append(
                        jnp.take_along_axis(line, lane_at[h], axis=1, wrap_negative_indices=False)
                    )
            for h in halves:
                level_found, bit = found[h], 1
                while len(level_found) > 1:
                    odd = (row_at[h] & bit) > 0
                    level_found = [
                        jnp.where(odd, level_found[j + 1], level_found[j])
                        for j in range(0, len(level_found), 2)
                    ]
                    bit *= 2
                take(h, at, level_found[0])

        over(0, rows // 8, body)

    for turn in range(ITERS):
        inner(velocity_rows)
        take_map(S_PLAN)
        beside(velocity_rows)
        take_depth(S_PLAN)
        outer(velocity_rows)
        if turn == ITERS - 1:
            @pl.when(d == 0)
            def _():
                tiles[1] = V[2, 2, xs, :]
            send_tile(1)
        send_depth(V_PLAN)
        send_map(V_PLAN)
        if turn < ITERS - 1:
            @pl.when(d == 0)
            def _():
                now = time_step * V[2, 2, xs, :]
                tiles[0] = now if turn == 0 else tiles[0] + now
            if turn == ITERS - 2:
                send_tile(0)
        wait_sends(S_PLAN)
        if turn == 0:
            ocean_fixed()
        inner(stress_rows)
        if turn == ITERS - 1:
            break
        take_map(V_PLAN)
        beside(stress_rows)
        take_depth(V_PLAN)
        outer(stress_rows)
        send_depth(S_PLAN)
        send_map(S_PLAN)
        wait_sends(V_PLAN)
        if turn == ITERS - 2:
            take_tile(0)
            def keep(h, at, found):
                lift2[h, at, :] = found

            pick(0, keep)

    v_store = pltpu.make_async_copy(V.at[:, pl.ds(2, nz), xs, :], vel_out, out_sem.at[0])
    v_store.start()

    take_tile(1)
    def begin(h, at, rate):
        here = pl.ds(at.start + 8, 8)
        w = W[h, here, :]
        level[0, h, here, :] = w * (height[h, at, :] + (lift2[h, at, :] + time_step * rate))
        source[h, at, :] = w * rate

    pick(1, begin)
    levels = [
        row_copies(level.at[t], 8 + 4 * t, True) + col_copies(3 + t, 10 + 4 * t, True)
        for t in range(OSTEPS)
    ]

    def send_level(t):
        col_send[3 + t] = jnp.where(first, level[t, 0, own, :], level[t, 1, own, :]).T
        start_all(levels[t])

    send_level(0)

    take_map(V_PLAN)
    beside(stress_rows)
    take_depth(V_PLAN)
    outer(stress_rows)
    s_store = pltpu.make_async_copy(S.at[:, pl.ds(2, nz), xs, :], str_out, out_sem.at[1])
    s_store.start()
    wait_sends(V_PLAN)

    for turn in range(OSTEPS):
        recv_all(levels[turn])
        sent_all(levels[turn])
        edge = col_recv[3 + turn].T
        L = level.at[turn]
        now = (L[0, own, :], L[1, own, :])
        ahead = east_of(now[0], now[1], edge)
        qw[...] = qw[...] - pull * hw[...] * (turn_lanes(now[0], -1) - edge)
        for h in halves:
            qx[h] = qx[h] - pull * hx[h] * (ahead[h] - now[h])
            qy[h] = qy[h] - pull * hy[h] * (
                L[h, pl.ds(1, rows + 8), :] - L[h, pl.ds(0, rows + 8), :]
            )
        behind = west_of(qx[0], qx[1], qw[...])
        for h in halves:
            new = (
                now[h]
                - ocean_step
                * W[h, own, :]
                * (
                    (qx[h] - behind[h])
                    + (qy[h, own, :] - qy[h, pl.ds(7, rows), :])
                )
                + ocean_step * source[h]
            )
            if turn < OSTEPS - 1:
                level[turn + 1, h, own, :] = new
            else:
                height[h] = new
        if turn < OSTEPS - 1:
            send_level(turn + 1)

    stores = []
    for h in halves:
        cols = pl.ds(h * LANES, LANES)
        for src, dst in (
            (height.at[h], height_out.at[:, cols]),
            (qx.at[h], disch_out.at[0, :, cols]),
            (qy.at[h, own, :], disch_out.at[1, :, cols]),
        ):
            stores.append(pltpu.make_async_copy(src, dst, out_sem.at[2 + len(stores)]))
            stores[-1].start()
    if n_depth > 1:
        for k in range(2):
            each(d == 0, sends[k], "wait_send")
    for c in [v_store, s_store] + stores:
        c.wait()


def solution(mesh):
    n_depth, n_map = mesh.shape["depth"], mesh.shape["map"]

    def per_device(*args):
        velocity, stress, height, discharge = args[0], args[1], args[6], args[7]
        nz, nx = velocity.shape[1], velocity.shape[2]
        rows = height.shape[0]
        f32 = jnp.float32
        hbm = pl.BlockSpec(memory_space=pltpu.HBM)
        any_space = pl.BlockSpec(memory_space=pl.ANY)

        def vm(*shape, dtype=f32):
            return pltpu.VMEM(shape, dtype)

        halves = vm(2, rows, LANES)
        ints = vm(2, rows, LANES, dtype=jnp.int32)
        low_pad = vm(2, rows + 8, LANES)
        padded = vm(2, rows + 16, LANES)
        n_up = len(up_slots(S_MAP))
        n_down = len(down_slots(S_MAP))
        n_vup = len(up_slots(V_MAP))
        n_vdown = len(down_slots(V_MAP))
        dma = pltpu.SemaphoreType.DMA
        scratch = [
            vm(6, nz + 4, nx + 16, LANES),
            vm(3, nz + 4, nx + 16, LANES),
            vm(nz, nx, LANES, dtype=jnp.int32),
            vm(nz, nx, LANES),
            vm(nz, nx, LANES),
            vm(nz, nx, LANES),
            vm(n_up, nz, LANES),
            vm(n_down, nz, LANES),
            vm(n_up, nz, LANES),
            vm(n_down, nz, LANES),
            vm(n_vup, nz, LANES),
            vm(n_vdown, nz, LANES),
            vm(n_vup, nz, LANES),
            vm(n_vdown, nz, LANES),
            vm(2, nx, LANES),
            vm(OSTEPS, 2, rows + 16, LANES),
            padded,
            ints,
            ints,
            halves,
            halves,
            halves,
            halves,
            low_pad,
            low_pad,
            low_pad,
            halves,
            halves,
            vm(3 + OSTEPS, LANES, LANES),
            vm(3 + OSTEPS, LANES, LANES),
            vm(LANES, LANES),
            vm(LANES, LANES),
        ]
        scratch += [pltpu.SMEM(args[k].shape, f32) for k in (3, 4, 5)]
        scratch += [
            dma((28,)),
            dma((8,)),
            dma((6,)),
            dma((6,)),
            dma((6,)),
            dma((6,)),
            dma((2 * max(n_depth - 1, 1),)),
            dma((2,)),
            dma((8 + 4 * OSTEPS,)),
            dma((8 + 4 * OSTEPS,)),
        ]

        def body(*refs):
            kernel(n_depth, n_map, nz, nx, rows, *refs)

        shapes = tuple(
            jax.ShapeDtypeStruct(x.shape, f32) for x in (velocity, stress, height, discharge)
        )
        results = pl.pallas_call(
            body,
            out_shape=shapes,
            in_specs=[hbm] * len(args),
            out_specs=(any_space,) * 4,
            scratch_shapes=scratch,
            compiler_params=pltpu.CompilerParams(
                collective_id=0, has_side_effects=True, vmem_limit_bytes=32 * 1024 * 1024
            ),
        )(*[pltpu.with_memory_space_constraint(x, pltpu.HBM) for x in args])

        def deliver(*refs):
            copies = [
                pltpu.make_async_copy(refs[k], refs[4 + k], refs[8].at[k]) for k in range(4)
            ]
            for c in copies:
                c.start()
            for c in copies:
                c.wait()

        return pl.pallas_call(
            deliver,
            out_shape=shapes,
            in_specs=[any_space] * 4,
            out_specs=(hbm,) * 4,
            scratch_shapes=[dma((4,))],
            compiler_params=pltpu.CompilerParams(vmem_limit_bytes=1024 * 1024),
        )(*results)

    return jax.shard_map(
        per_device,
        mesh=mesh,
        in_specs=(
            P(None, "depth", "map", None),
            P(None, "depth", "map", None),
            P("depth", "map", None),
            P(),
            P(),
            P(),
            P("depth", "map"),
            P(None, "depth", "map"),
            P(None, "depth", "map"),
            P("depth", "map"),
            P("depth", "map"),
        ),
        out_specs=(
            P(None, "depth", "map", None),
            P(None, "depth", "map", None),
            P("depth", "map"),
            P(None, "depth", "map"),
        ),
        check_vma=False,
    )
```

```python
import jax
import jax.numpy as jnp
from jax import lax
from jax.experimental import pallas as pl
from jax.experimental.pallas import tpu as pltpu
from jax.sharding import PartitionSpec as P

ITERS = 3
OSTEPS = 2

far_coef = 1.0 / 24.0
RATIO = 27.0
time_step = 0.2
ocean_step = 0.2
gravity = 1.0
pull = ocean_step * gravity

LANES = 128
ROW0 = 8
XX, XY, XZ, YZ, ZZ, YY = range(6)
S_DEPTH = ((XZ, YZ + 1, True), (ZZ, ZZ + 1, False))
V_DEPTH = ((0, 2, False), (2, 3, True))
S_MAP = ((XX, False), (XY, True), (XZ, True))
V_MAP = ((0, True), (1, False), (2, False))


def turn_lanes(x, by):
    return pltpu.roll(x, by % LANES, 1)


def fwd(p1, c, p2, m1):
    return p1 - c, p2 - m1


def bwd(c, m1, p1, m2):
    return c - m1, p1 - m2


def fwd_y(f):
    return fwd(turn_lanes(f, -1), f, turn_lanes(f, -2), turn_lanes(f, 1))


def bwd_y(f):
    return bwd(f, turn_lanes(f, 1), turn_lanes(f, -1), turn_lanes(f, 2))


def scaled(*pairs):
    near, far = pairs[0]
    for n, f in pairs[1:]:
        near, far = near + n, far + f
    return RATIO * near - far


def up_slots(fields):
    out = []
    for field, back in fields:
        for k in (2, 1) if back else (1,):
            out.append((field, -k, -k))
    return out


def down_slots(fields):
    out = []
    for field, back in fields:
        for k in (0,) if back else (0, 1):
            out.append((field, k, k))
    return out


N_ROWS = 9


def kernel(
    n_depth,
    n_map,
    nz,
    nx,
    rows,
    vel_in,
    str_in,
    reg_in,
    lame_in,
    shear_in,
    buoy_in,
    height_in,
    disch_in,
    face_in,
    wet_in,
    index_in,
    vel_out,
    str_out,
    height_out,
    disch_out,
    S,
    V,
    region,
    dtb,
    dtl,
    dts,
    s_mid,
    s_end,
    v_mid,
    v_end,
    tiles,
    level,
    W,
    wet_i,
    index,
    height,
    qx,
    hx,
    fd0,
    qy,
    hy,
    fd1,
    source,
    lift2,
    col_send,
    col_recv,
    qw,
    hw,
    lame_t,
    shear_t,
    buoy_t,
    in_sem,
    out_sem,
    s_send_sem,
    s_recv_sem,
    v_send_sem,
    v_recv_sem,
    t_send_sem,
    t_recv_sem,
    o_send_sem,
    o_recv_sem,
):
    d = lax.axis_index("depth")
    m = lax.axis_index("map")
    has_low, has_high = d > 0, d < n_depth - 1
    has_west, has_east = m > 0, m < n_map - 1
    low, high = {"depth": d - 1, "map": m}, {"depth": d + 1, "map": m}
    west, east = {"depth": d, "map": m - 1}, {"depth": d, "map": m + 1}
    sides = ((has_low, low), (has_high, high), (has_west, west), (has_east, east))
    f32 = jnp.float32
    halves = range(2)

    s_loads = [
        pltpu.make_async_copy(
            str_in.at[f], S.at[f, pl.ds(2, nz), pl.ds(ROW0, nx), :], in_sem.at[f]
        )
        for f in range(6)
    ]
    r_loads = [
        pltpu.make_async_copy(src, dst, in_sem.at[k])
        for src, dst, k in (
            (reg_in, region, 6),
            (lame_in, lame_t, 24),
            (shear_in, shear_t, 25),
            (buoy_in, buoy_t, 26),
        )
    ]
    v_loads = [
        pltpu.make_async_copy(
            vel_in.at[f], V.at[f, pl.ds(2, nz), pl.ds(ROW0, nx), :], in_sem.at[7 + f]
        )
        for f in range(3)
    ]
    o_loads = []

    def half_load(src, dst):
        o_loads.append(pltpu.make_async_copy(src, dst, in_sem.at[10 + len(o_loads)]))

    for h in halves:
        cols = pl.ds(h * LANES, LANES)
        half_load(wet_in.at[:, cols], wet_i.at[h])
        half_load(index_in.at[:, cols], index.at[h])
        half_load(height_in.at[:, cols], height.at[h])
        half_load(disch_in.at[0, :, cols], qx.at[h])
        half_load(disch_in.at[1, :, cols], qy.at[h, pl.ds(8, rows), :])
        half_load(face_in.at[0, :, cols], fd0.at[h])
        half_load(face_in.at[1, :, cols], fd1.at[h, pl.ds(8, rows), :])
    for c in s_loads + r_loads + v_loads + o_loads:
        c.start()

    def clear_layers(z):
        for f in (XZ, YZ, ZZ):
            S[f, pl.ds(z, 2), pl.ds(ROW0, nx), :] = jnp.zeros((2, nx, LANES), f32)
        for f in range(3):
            V[f, pl.ds(z, 2), pl.ds(ROW0, nx), :] = jnp.zeros((2, nx, LANES), f32)

    @pl.when(d == 0)
    def _():
        clear_layers(0)

    @pl.when(d == n_depth - 1)
    def _():
        clear_layers(nz + 2)

    for there in (m == 0, m == n_map - 1):
        @pl.when(there)
        def _():
            for ref in (s_mid, s_end, v_mid, v_end):
                for j in range(N_ROWS):
                    ref[1, j] = jnp.zeros(ref.shape[2:], f32)

    for h in halves:
        for t in range(OSTEPS):
            level[t, h, pl.ds(0, 8), :] = jnp.zeros((8, LANES), f32)
            level[t, h, pl.ds(rows + 8, 8), :] = jnp.zeros((8, LANES), f32)
        W[h, pl.ds(0, 8), :] = jnp.zeros((8, LANES), f32)
        W[h, pl.ds(rows + 8, 8), :] = jnp.zeros((8, LANES), f32)
        qy[h, pl.ds(0, 8), :] = jnp.zeros((8, LANES), f32)
        fd1[h, pl.ds(0, 8), :] = jnp.zeros((8, LANES), f32)
    for k in range(3 + OSTEPS):
        col_recv[k] = jnp.zeros((LANES, LANES), f32)

    barrier = pltpu.get_barrier_semaphore()
    for there, who in sides:
        @pl.when(there)
        def _():
            pl.semaphore_signal(barrier, inc=1, device_id=who, device_id_type=pl.DeviceIdType.MESH)

    @pl.when(d > 1)
    def _():
        pl.semaphore_signal(
            barrier, inc=1, device_id={"depth": 0, "map": m}, device_id_type=pl.DeviceIdType.MESH
        )

    peers = sum(there.astype(jnp.int32) for there, _who in sides)
    pl.semaphore_wait(barrier, peers + jnp.where(d == 0, max(n_depth - 2, 0), 0))

    def remote(src, dst, ssem, rsem, who):
        return pltpu.make_async_remote_copy(
            src_ref=src,
            dst_ref=dst,
            send_sem=ssem,
            recv_sem=rsem,
            device_id=who,
            device_id_type=pl.DeviceIdType.MESH,
        )

    def over(lo, hi, body, at_once=1):
        def step(i, _):
            for k in range(at_once):
                body(lo + i * at_once + k)
            return 0

        lax.fori_loop(0, (hi - lo) // at_once, step, 0)

    xs = pl.ds(ROW0, nx)

    def depth_copies(ref, fields, ssem, rsem):
        ups, downs = [], []
        for k, (lo, hi, back) in enumerate(fields):
            n_up, n_down = (2, 1) if back else (1, 2)
            fs = pl.ds(lo, hi - lo)
            ups.append(
                remote(
                    ref.at[fs, pl.ds(nz + 2 - n_up, n_up), xs, :],
                    ref.at[fs, pl.ds(2 - n_up, n_up), xs, :],
                    ssem.at[k],
                    rsem.at[k],
                    high,
                )
            )
            downs.append(
                remote(
                    ref.at[fs, pl.ds(2, n_down), xs, :],
                    ref.at[fs, pl.ds(nz + 2, n_down), xs, :],
                    ssem.at[2 + k],
                    rsem.at[2 + k],
                    low,
                )
            )
        return ups, downs

    s_up, s_down = depth_copies(S, S_DEPTH, s_send_sem, s_recv_sem)
    v_up, v_down = depth_copies(V, V_DEPTH, v_send_sem, v_recv_sem)

    def map_copies(fields, buf, ssem, rsem, k):
        n_up = len(up_slots(fields))
        ups, downs = pl.ds(0, n_up), pl.ds(n_up, N_ROWS - n_up)
        return (
            [remote(buf.at[0, ups], buf.at[1, ups], ssem.at[k], rsem.at[k], east)],
            [remote(buf.at[0, downs], buf.at[1, downs], ssem.at[k + 1], rsem.at[k + 1], west)],
        )

    end_layers = [0, 1, nz - 2, nz - 1]
    S_PLAN = dict(ref=S, fields=S_MAP, up=s_up, down=s_down)
    S_PLAN["mid"] = (s_mid, map_copies(S_MAP, s_mid, s_send_sem, s_recv_sem, 4))
    S_PLAN["end"] = (s_end, map_copies(S_MAP, s_end, s_send_sem, s_recv_sem, 6))
    V_PLAN = dict(ref=V, fields=V_MAP, up=v_up, down=v_down)
    V_PLAN["mid"] = (v_mid, map_copies(V_MAP, v_mid, v_send_sem, v_recv_sem, 4))
    V_PLAN["end"] = (v_end, map_copies(V_MAP, v_end, v_send_sem, v_recv_sem, 6))

    def each(there, copies, what):
        @pl.when(there)
        def _():
            for c in copies:
                getattr(c, what)()

    def send_depth(plan):
        each(has_high, plan["up"], "start")
        each(has_low, plan["down"], "start")

    def over_layers(part, body):
        if part == "mid":
            over(2, nz - 2, lambda z: body(z, z - 2), 4)
        else:
            for i, z in enumerate(end_layers):
                body(z, i)

    def send_map(plan, part):
        ref, (buf, (eastward, westward)) = plan["ref"], plan[part]
        n_up = len(up_slots(plan["fields"]))

        def pack(z, i):
            for j, (f, row, _r) in enumerate(up_slots(plan["fields"])):
                buf[0, j, pl.ds(i, 1), :] = ref[f, z + 2, pl.ds(ROW0 + nx + row, 1), :]
            for j, (f, row, _r) in enumerate(down_slots(plan["fields"])):
                buf[0, n_up + j, pl.ds(i, 1), :] = ref[f, z + 2, pl.ds(ROW0 + row, 1), :]

        over_layers(part, pack)
        each(has_east, eastward, "start")
        each(has_west, westward, "start")

    def take_map(plan, part):
        ref, (buf, (eastward, westward)) = plan["ref"], plan[part]
        n_up = len(up_slots(plan["fields"]))
        each(has_west, eastward, "wait_recv")
        each(has_east, westward, "wait_recv")

        def unpack(z, i):
            for j, (f, _row, row) in enumerate(up_slots(plan["fields"])):
                ref[f, z + 2, pl.ds(ROW0 + row, 1), :] = buf[1, j, pl.ds(i, 1), :]
            for j, (f, _row, row) in enumerate(down_slots(plan["fields"])):
                ref[f, z + 2, pl.ds(ROW0 + nx + row, 1), :] = buf[1, n_up + j, pl.ds(i, 1), :]

        over_layers(part, unpack)

    def take_low(plan):
        each(has_low, plan["up"], "wait_recv")

    def take_high(plan):
        each(has_high, plan["down"], "wait_recv")

    def wait_sends(plan):
        each(has_high, plan["up"], "wait_send")
        each(has_low, plan["down"], "wait_send")
        for part in ("mid", "end"):
            each(has_east, plan[part][1][0], "wait_send")
            each(has_west, plan[part][1][1], "wait_send")

    def velocity_rows(z, a, b, along):
        def s(f, dz, dx):
            return S[f, z + 2 + dz, pl.ds(ROW0 + a + dx, b - a), :]

        parts = [[], [], []]
        if "y" in along:
            parts[0].append(bwd_y(s(XY, 0, 0)))
            parts[1].append(fwd_y(s(YY, 0, 0)))
            parts[2].append(bwd_y(s(YZ, 0, 0)))
        if "x" in along:
            parts[0].append(fwd(s(XX, 0, 1), s(XX, 0, 0), s(XX, 0, 2), s(XX, 0, -1)))
            parts[1].append(bwd(s(XY, 0, 0), s(XY, 0, -1), s(XY, 0, 1), s(XY, 0, -2)))
            parts[2].append(bwd(s(XZ, 0, 0), s(XZ, 0, -1), s(XZ, 0, 1), s(XZ, 0, -2)))
        if "z" in along:
            parts[0].append(bwd(s(XZ, 0, 0), s(XZ, -1, 0), s(XZ, 1, 0), s(XZ, -2, 0)))
            parts[1].append(bwd(s(YZ, 0, 0), s(YZ, -1, 0), s(YZ, 1, 0), s(YZ, -2, 0)))
            parts[2].append(fwd(s(ZZ, 1, 0), s(ZZ, 0, 0), s(ZZ, 2, 0), s(ZZ, -1, 0)))
        scale = dtb[z, pl.ds(a, b - a), :]
        for f in range(3):
            at = (f, z + 2, pl.ds(ROW0 + a, b - a), slice(None))
            V[at] = V[at] + scale * scaled(*parts[f])

    def stress_rows(z, a, b, along):
        def v(f, dz, dx):
            return V[f, z + 2 + dz, pl.ds(ROW0 + a + dx, b - a), :]

        x, y, w = v(0, 0, 0), v(1, 0, 0), v(2, 0, 0)
        own = {}
        shears = {XY: [], XZ: [], YZ: []}
        if "y" in along:
            own[YY] = scaled(bwd_y(y))
            shears[XY].append(fwd_y(x))
            shears[YZ].append(fwd_y(w))
        if "x" in along:
            own[XX] = scaled(bwd(x, v(0, 0, -1), v(0, 0, 1), v(0, 0, -2)))
            shears[XY].append(fwd(v(1, 0, 1), y, v(1, 0, 2), v(1, 0, -1)))
            shears[XZ].append(fwd(v(2, 0, 1), w, v(2, 0, 2), v(2, 0, -1)))
        if "z" in along:
            own[ZZ] = scaled(bwd(w, v(2, -1, 0), v(2, 1, 0), v(2, -2, 0)))
            shears[XZ].append(fwd(v(0, 1, 0), x, v(0, 2, 0), v(0, -1, 0)))
            shears[YZ].append(fwd(v(1, 1, 0), y, v(1, 2, 0), v(1, -1, 0)))
        mu = dts[z, pl.ds(a, b - a), :]
        both = dtl[z, pl.ds(a, b - a), :] * sum(list(own.values())[1:], list(own.values())[0])
        mu2 = mu + mu
        changes = {f: both + mu2 * own[f] if f in own else both for f in (XX, YY, ZZ)}
        changes.update({f: mu * scaled(*p) for f, p in shears.items() if p})
        for f, change in changes.items():
            at = (f, z + 2, pl.ds(ROW0 + a, b - a), slice(None))
            S[at] = S[at] + change

    def local(rows_of):
        def body(z, along):
            rows_of(z, 0, 8, along)
            rows_of(z, 8, nx - 8, along + "x")
            rows_of(z, nx - 8, nx, along)

        over(2, nz - 2, lambda z: body(z, "yz"))

        def ends(i):
            body(i, "y")
            body(i + nz - 2, "y")

        over(0, 2, ends)

    def after_map(rows_of, part):
        def body(z):
            rows_of(z, 0, 8, "x")
            rows_of(z, nx - 8, nx, "x")

        if part == "mid":
            over(2, nz - 2, body, 2)
        else:
            over(0, 2, body)
            over(nz - 2, nz, body)

    def after_low(rows_of):
        over(0, 2, lambda z: rows_of(z, 0, nx, "z"))

    def after_high(rows_of):
        over(nz - 2, nz, lambda z: rows_of(z, 0, nx, "z"))

    for c in s_loads:
        c.wait()
    send_map(S_PLAN, "mid")
    send_map(S_PLAN, "end")
    send_depth(S_PLAN)

    for c in r_loads:
        c.wait()
    lame = [lame_t[k] * (time_step * far_coef) for k in range(8)]
    shear = [shear_t[k] * (time_step * far_coef) for k in range(8)]
    buoy = [buoy_t[k] * (time_step * far_coef) for k in range(8)]

    def material(z):
        r = region[z]
        bit0, bit1, bit2 = (r & 1) > 0, (r & 2) > 0, (r & 4) > 0
        for table, out in ((lame, dtl), (shear, dts), (buoy, dtb)):
            a = [jnp.where(bit0, table[2 * k + 1], table[2 * k]) for k in range(4)]
            b = [jnp.where(bit1, a[2 * k + 1], a[2 * k]) for k in range(2)]
            out[z] = jnp.where(bit2, b[1], b[0])

    over(0, nz, material)
    for c in v_loads:
        c.wait()

    lane = lax.broadcasted_iota(jnp.int32, (rows, LANES), 1)
    first, last = lane == 0, lane == LANES - 1
    own = pl.ds(8, rows)

    def row_copies(ref, k, both):
        out = [
            (
                has_high,
                has_low,
                remote(
                    ref.at[:, pl.ds(rows, 8), :],
                    ref.at[:, pl.ds(0, 8), :],
                    o_send_sem.at[k],
                    o_recv_sem.at[k],
                    high,
                ),
            )
        ]
        if both:
            out.append(
                (
                    has_low,
                    has_high,
                    remote(
                        ref.at[:, pl.ds(8, 8), :],
                        ref.at[:, pl.ds(rows + 8, 8), :],
                        o_send_sem.at[k + 1],
                        o_recv_sem.at[k + 1],
                        low,
                    ),
                )
            )
        return out

    def col_copies(slot, k, both):
        tail = pl.ds(LANES - 8, 8)
        out = [
            (
                has_east,
                has_west,
                remote(
                    col_send.at[slot, tail, :],
                    col_recv.at[slot, tail, :],
                    o_send_sem.at[k],
                    o_recv_sem.at[k],
                    east,
                ),
            )
        ]
        if both:
            head = pl.ds(0, 8)
            out.append(
                (
                    has_west,
                    has_east,
                    remote(
                        col_send.at[slot, head, :],
                        col_recv.at[slot, head, :],
                        o_send_sem.at[k + 1],
                        o_recv_sem.at[k + 1],
                        west,
                    ),
                )
            )
        return out

    def start_all(copies):
        for there, _from, c in copies:
            each(there, [c], "start")

    def recv_all(copies):
        for _there, came, c in copies:
            each(came, [c], "wait_recv")

    def sent_all(copies):
        for there, _from, c in copies:
            each(there, [c], "wait_send")

    for c in o_loads:
        c.wait()
    for h in halves:
        W[h, own, :] = wet_i[h].astype(f32)
    col_send[0] = jnp.where(first, W[0, own, :], W[1, own, :]).T
    col_send[1] = fd0[1].T
    col_send[2] = qx[1].T
    fixed = (
        row_copies(W, 0, True)
        + row_copies(fd1, 2, False)
        + row_copies(qy, 3, False)
        + col_copies(0, 4, True)
        + col_copies(1, 6, False)
        + col_copies(2, 7, False)
    )
    start_all(fixed)

    def east_of(x0, x1, edge):
        r1 = turn_lanes(x1, -1)
        return (
            jnp.where(last, r1, turn_lanes(x0, -1)),
            jnp.where(last, turn_lanes(edge, -1), r1),
        )

    def west_of(x0, x1, edge):
        r0 = turn_lanes(x0, 1)
        return (
            jnp.where(first, turn_lanes(edge, 1), r0),
            jnp.where(first, r0, turn_lanes(x1, 1)),
        )

    def ocean_fixed():
        recv_all(fixed)
        sent_all(fixed)
        edge = col_recv[0].T
        w = (W[0, own, :], W[1, own, :])
        w_east = east_of(w[0], w[1], edge)
        wide = pl.ds(0, rows + 8)
        for h in halves:
            mask = w[h] * w_east[h]
            hx[h] = fd0[h] * mask
            qx[h] = qx[h] * mask
            mask = W[h, wide, :] * W[h, pl.ds(1, rows + 8), :]
            hy[h] = fd1[h] * mask
            qy[h] = qy[h] * mask
        mask = edge * turn_lanes(w[0], -1)
        hw[...] = col_recv[1].T * mask
        qw[...] = col_recv[2].T * mask

    def tile_copies(k):
        return [
            remote(
                tiles.at[k],
                tiles.at[k],
                t_send_sem.at[k * (n_depth - 1) + i],
                t_recv_sem.at[k],
                {"depth": i + 1, "map": m},
            )
            for i in range(n_depth - 1)
        ]

    sends = [tile_copies(0), tile_copies(1)]

    def send_tile(k):
        if n_depth > 1:
            each(d == 0, sends[k], "start")

    def take_tile(k):
        if n_depth > 1:
            each(d > 0, sends[k][:1], "wait_recv")

    def pick(k, take):
        def body(i):
            at = pl.ds(i * 8, 8)
            where = [index[h, at, :] for h in halves]
            lane_at = [x & (LANES - 1) for x in where]
            row_at = [x >> 7 for x in where]
            found = [[], []]
            for r in range(nx):
                line = jnp.broadcast_to(tiles[k, pl.ds(r, 1), :], (8, LANES))
                for h in halves:
                    found[h].append(
                        jnp.take_along_axis(line, lane_at[h], axis=1, wrap_negative_indices=False)
                    )
            for h in halves:
                level_found, bit = found[h], 1
                while len(level_found) > 1:
                    odd = (row_at[h] & bit) > 0
                    level_found = [
                        jnp.where(odd, level_found[j + 1], level_found[j])
                        for j in range(0, len(level_found), 2)
                    ]
                    bit *= 2
                take(h, at, level_found[0])

        over(0, rows // 8, body, 2)

    for turn in range(ITERS):
        local(velocity_rows)
        take_map(S_PLAN, "mid")
        after_map(velocity_rows, "mid")
        send_map(V_PLAN, "mid")
        take_map(S_PLAN, "end")
        after_map(velocity_rows, "end")
        take_low(S_PLAN)
        after_low(velocity_rows)
        if turn == ITERS - 1:
            @pl.when(d == 0)
            def _():
                tiles[1] = V[2, 2, xs, :]
            send_tile(1)
        take_high(S_PLAN)
        after_high(velocity_rows)
        send_map(V_PLAN, "end")
        send_depth(V_PLAN)
        if turn < ITERS - 1:
            @pl.when(d == 0)
            def _():
                now = time_step * V[2, 2, xs, :]
                tiles[0] = now if turn == 0 else tiles[0] + now
            if turn == ITERS - 2:
                send_tile(0)
        wait_sends(S_PLAN)
        local(stress_rows)
        if turn == 0:
            ocean_fixed()
        if turn == ITERS - 1:
            break
        take_map(V_PLAN, "mid")
        after_map(stress_rows, "mid")
        send_map(S_PLAN, "mid")
        take_map(V_PLAN, "end")
        after_map(stress_rows, "end")
        take_low(V_PLAN)
        after_low(stress_rows)
        take_high(V_PLAN)
        after_high(stress_rows)
        send_map(S_PLAN, "end")
        send_depth(S_PLAN)
        wait_sends(V_PLAN)
        if turn == ITERS - 2:
            take_tile(0)

            def keep(h, at, found):
                lift2[h, at, :] = found

            pick(0, keep)

    v_store = pltpu.make_async_copy(V.at[:, pl.ds(2, nz), xs, :], vel_out, out_sem.at[0])
    v_store.start()

    take_tile(1)
    def begin(h, at, rate):
        here = pl.ds(at.start + 8, 8)
        w = W[h, here, :]
        level[0, h, here, :] = w * (height[h, at, :] + (lift2[h, at, :] + time_step * rate))
        source[h, at, :] = w * rate

    pick(1, begin)
    levels = [
        row_copies(level.at[t], 8 + 4 * t, True) + col_copies(3 + t, 10 + 4 * t, True)
        for t in range(OSTEPS)
    ]

    def send_level(t):
        col_send[3 + t] = jnp.where(first, level[t, 0, own, :], level[t, 1, own, :]).T
        start_all(levels[t])

    send_level(0)

    for part in ("mid", "end"):
        take_map(V_PLAN, part)
        after_map(stress_rows, part)
    take_low(V_PLAN)
    after_low(stress_rows)
    take_high(V_PLAN)
    after_high(stress_rows)
    s_store = pltpu.make_async_copy(S.at[:, pl.ds(2, nz), xs, :], str_out, out_sem.at[1])
    s_store.start()
    wait_sends(V_PLAN)

    for turn in range(OSTEPS):
        L = level.at[turn]
        now = (L[0, own, :], L[1, own, :])

        def flow_x(h, ahead):
            qx[h] = qx[h] - pull * hx[h] * (ahead - now[h])

        def flow_y(at, n):
            for h in halves:
                here = pl.ds(at, n)
                qy[h, here, :] = qy[h, here, :] - pull * hy[h, here, :] * (
                    L[h, pl.ds(at + 1, n), :] - L[h, here, :]
                )

        flow_x(0, east_of(now[0], now[1], now[1])[0])
        flow_y(8, rows - 8)
        recv_all(levels[turn])
        edge = col_recv[3 + turn].T
        flow_x(1, east_of(now[0], now[1], edge)[1])
        flow_y(0, 8)
        flow_y(rows, 8)
        qw[...] = qw[...] - pull * hw[...] * (turn_lanes(now[0], -1) - edge)
        behind = west_of(qx[0], qx[1], qw[...])
        for h in halves:
            new = (
                now[h]
                - ocean_step
                * W[h, own, :]
                * (
                    (qx[h] - behind[h])
                    + (qy[h, own, :] - qy[h, pl.ds(7, rows), :])
                )
                + ocean_step * source[h]
            )
            if turn < OSTEPS - 1:
                level[turn + 1, h, own, :] = new
            else:
                height[h] = new
        if turn < OSTEPS - 1:
            send_level(turn + 1)

    stores = []
    for h in halves:
        cols = pl.ds(h * LANES, LANES)
        for src, dst in (
            (height.at[h], height_out.at[:, cols]),
            (qx.at[h], disch_out.at[0, :, cols]),
            (qy.at[h, own, :], disch_out.at[1, :, cols]),
        ):
            stores.append(pltpu.make_async_copy(src, dst, out_sem.at[2 + len(stores)]))
            stores[-1].start()
    for copies in levels:
        sent_all(copies)
    if n_depth > 1:
        for k in range(2):
            each(d == 0, sends[k], "wait_send")
    for c in [v_store, s_store] + stores:
        c.wait()


def solution(mesh):
    n_depth, n_map = mesh.shape["depth"], mesh.shape["map"]

    def per_device(*args):
        velocity, stress, height, discharge = args[0], args[1], args[6], args[7]
        nz, nx = velocity.shape[1], velocity.shape[2]
        rows = height.shape[0]
        f32 = jnp.float32
        hbm = pl.BlockSpec(memory_space=pltpu.HBM)
        any_space = pl.BlockSpec(memory_space=pl.ANY)

        def vm(*shape, dtype=f32):
            return pltpu.VMEM(shape, dtype)

        halves = vm(2, rows, LANES)
        ints = vm(2, rows, LANES, dtype=jnp.int32)
        low_pad = vm(2, rows + 8, LANES)
        padded = vm(2, rows + 16, LANES)
        dma = pltpu.SemaphoreType.DMA
        scratch = [
            vm(6, nz + 4, nx + 16, LANES),
            vm(3, nz + 4, nx + 16, LANES),
            vm(nz, nx, LANES, dtype=jnp.int32),
            vm(nz, nx, LANES),
            vm(nz, nx, LANES),
            vm(nz, nx, LANES),
            vm(2, N_ROWS, nz - 4, LANES),
            vm(2, N_ROWS, 4, LANES),
            vm(2, N_ROWS, nz - 4, LANES),
            vm(2, N_ROWS, 4, LANES),
            vm(2, nx, LANES),
            vm(OSTEPS, 2, rows + 16, LANES),
            padded,
            ints,
            ints,
            halves,
            halves,
            halves,
            halves,
            low_pad,
            low_pad,
            low_pad,
            halves,
            halves,
            vm(3 + OSTEPS, LANES, LANES),
            vm(3 + OSTEPS, LANES, LANES),
            vm(LANES, LANES),
            vm(LANES, LANES),
        ]
        scratch += [pltpu.SMEM(args[k].shape, f32) for k in (3, 4, 5)]
        scratch += [
            dma((28,)),
            dma((8,)),
            dma((8,)),
            dma((8,)),
            dma((8,)),
            dma((8,)),
            dma((2 * max(n_depth - 1, 1),)),
            dma((2,)),
            dma((8 + 4 * OSTEPS,)),
            dma((8 + 4 * OSTEPS,)),
        ]

        def body(*refs):
            kernel(n_depth, n_map, nz, nx, rows, *refs)

        shapes = tuple(
            jax.ShapeDtypeStruct(x.shape, f32) for x in (velocity, stress, height, discharge)
        )
        results = pl.pallas_call(
            body,
            out_shape=shapes,
            in_specs=[hbm] * len(args),
            out_specs=(any_space,) * 4,
            scratch_shapes=scratch,
            compiler_params=pltpu.CompilerParams(
                collective_id=0, has_side_effects=True, vmem_limit_bytes=32 * 1024 * 1024
            ),
        )(*[pltpu.with_memory_space_constraint(x, pltpu.HBM) for x in args])

        def deliver(*refs):
            copies = [
                pltpu.make_async_copy(refs[k], refs[4 + k], refs[8].at[k]) for k in range(4)
            ]
            for c in copies:
                c.start()
            for c in copies:
                c.wait()

        return pl.pallas_call(
            deliver,
            out_shape=shapes,
            in_specs=[any_space] * 4,
            out_specs=(hbm,) * 4,
            scratch_shapes=[dma((4,))],
            compiler_params=pltpu.CompilerParams(vmem_limit_bytes=1024 * 1024),
        )(*results)

    return jax.shard_map(
        per_device,
        mesh=mesh,
        in_specs=(
            P(None, "depth", "map", None),
            P(None, "depth", "map", None),
            P("depth", "map", None),
            P(),
            P(),
            P(),
            P("depth", "map"),
            P(None, "depth", "map"),
            P(None, "depth", "map"),
            P("depth", "map"),
            P("depth", "map"),
        ),
        out_specs=(
            P(None, "depth", "map", None),
            P(None, "depth", "map", None),
            P("depth", "map"),
            P(None, "depth", "map"),
        ),
        check_vma=False,
    )
```
